32 devices in a mesh: vec: 4 (over y, x), orb: 8 (over z, core).
Axes of the slice: x: 2, y: 2, z: 4, core: 2. Of those that a mesh axis runs over, the one named last changes fastest.
Arguments:
- chol_occ: float32 [44, 96, 1056], P('vec', 'orb'), may hold values from -6 to 6
- chol_vir: float32 [44, 960, 1056], P('vec', 'orb'), may hold values from -6 to 6
- singles: float32 [96, 960], P('orb'), may hold values from -0.6 to 0.6
Outputs:
- dressed_vir: float32 [44, 960, 1056], P('vec', 'orb')
- dressed_ov: float32 [44, 96, 960], P(None, 'orb', 'vec')
- fock_ov: float32 [96, 960], P('orb')
The draws below stay inside these ranges and needn't reach their ends.
All inputs are finite; a program needn't handle non-finite values.
Results may differ from the reference program's by a relative error of at most 0.000086.
Values sent between devices are 32-bit elements; how exact they have to be, the bound alone decides.
A program may use at most 64 MiB of HBM per device.

```python
import jax
import jax.numpy as jnp
from jax import lax

O = 96
V = 960
N = 1056
Q = 44


def block_scale(key, shape, shards, smallest, largest):
    level, own = 1.0, jax.random.fold_in(key, 6)
    for position, shards_of in shards:
        steps = jnp.exp(jax.random.uniform(jax.random.fold_in(own, position), (shards_of,), jnp.float32, smallest / len(shards), largest / len(shards)))
        level = level * jnp.repeat(steps, shape[position] // shards_of).reshape([-1 if axis == position else 1 for axis in range(len(shape))])
    return level


def bell_draw(own_key, extent, scale, most, cuts=(), kind=jnp.bfloat16):
    result = scale * jax.random.normal(own_key, extent, jnp.float32)
    if cuts:
        result = result * block_scale(own_key, extent, cuts, -0.22, 0.18)
    return jnp.clip(result, -most, most).astype(kind)


def setup_inputs(seed: int = 0) -> dict:
    key_list = jax.random.split(jax.random.key(seed), 4)
    return {
        "chol_occ": bell_draw(key_list[0], (Q, O, N), 1.0, 6.0, ((0, 4), (1, 8)), jnp.float32),
        "chol_vir": bell_draw(key_list[1], (Q, V, N), 1.0, 6.0, ((0, 4), (1, 8)), jnp.float32),
        "singles": bell_draw(key_list[2], (O, V), 0.1, 0.6, ((0, 8),), jnp.float32),
    }


def dress_right(matrix_rows, singles):
    occ_cols = matrix_rows[:, :, :O]
    extra_term = jnp.einsum("qrj,ja->qra", occ_cols, singles, precision=lax.Precision.HIGHEST)
    return jnp.concatenate([occ_cols, matrix_rows[:, :, O:] + extra_term], axis=2)


def reference(chol_occ, chol_vir, singles):
    singles_t = singles.T

    def one_vector(pair_input):
        occ_vector, vir_vector = pair_input
        left_rows = vir_vector - jnp.dot(singles_t, occ_vector, precision=lax.Precision.HIGHEST)
        return dress_right(left_rows[None], singles)[0]

    dressed_vir = lax.map(one_vector, (chol_occ, chol_vir))
    dressed_occ = dress_right(chol_occ, singles)
    dressed_ov = dressed_occ[:, :, O:]
    traces = jnp.trace(chol_occ[:, :, :O], axis1=1, axis2=2)
    fock_ov = jnp.einsum("q,qia->ia", traces, dressed_ov, precision=lax.Precision.HIGHEST) / Q
    return dressed_vir, dressed_ov, fock_ov
```

```python
import jax
import jax.numpy as jnp
from jax import lax
from jax.experimental import pallas as pl
from jax.experimental.pallas import tpu as pltpu
from jax.sharding import PartitionSpec as P

MESH = pl.DeviceIdType.MESH
F32, BF16 = jnp.float32, jnp.bfloat16
LANES = 128
CORES = 2


def split(x):
    hi = x.astype(BF16)
    return hi, (x - hi.astype(F32)).astype(BF16)


def dot(a, b):
    return jnp.dot(a, b, preferred_element_type=F32)


def make_kernel(W, D, Q, R, RV, N, A):
    OCC = N - A
    NZ = D // CORES
    GR = 8 if R % 8 == 0 else (4 if R % 4 == 0 else R)
    NJ = R // GR
    ROWS = Q * R
    GRAN = Q * NJ
    MAIN = N // LANES * LANES
    TAIL = N - MAIN
    SLOTS = LANES // TAIL if TAIL else 1
    GROUPS = -(-Q // SLOTS)
    PIECE = A // W
    KP = -(-OCC // LANES) * LANES
    UNITS = Q + 2

    def kernel(occ, vir, sing, out_vir, out_ov, out_fock,
               gath, amps, tails, vloc, oloc, sloc, xbuf, rows, drows, tmat, sleft,
               ovsend, ovrecv, ovout, fbuf, fout,
               s_right, s_left, s_part, r_sem, ov_s, ov_r, f_s, f_r, in_sem, v_in, v_out, o_out):
        v = lax.axis_index("vec")
        o = lax.axis_index("orb")
        z = o // CORES
        k = o % CORES
        has_r = z < NZ - 1
        has_l = z > 0
        right = lax.rem(o + CORES, D)
        left = lax.rem(o - CORES + D, D)
        part = z * CORES + (1 - k)

        c_occ = pltpu.make_async_copy(occ, oloc, in_sem.at[0])
        c_sing = pltpu.make_async_copy(sing, sloc, in_sem.at[1])
        c_occ.start()
        c_sing.start()

        def vin(q):
            return pltpu.make_async_copy(vir.at[q], vloc.at[q], v_in.at[q])

        def vout(q):
            return pltpu.make_async_copy(vloc.at[q], out_vir.at[q], v_out.at[q])

        @pl.loop(0, Q)
        def _(q):
            vin(q).start()

        bar = pltpu.get_barrier_semaphore()

        @pl.when(has_r)
        def _():
            pl.semaphore_signal(bar, inc=1, device_id=(v, right), device_id_type=MESH)

        @pl.when(has_l)
        def _():
            pl.semaphore_signal(bar, inc=1, device_id=(v, left), device_id_type=MESH)

        pl.semaphore_signal(bar, inc=1, device_id=(v, part), device_id_type=MESH)
        for h in range(1, W):
            pl.semaphore_signal(bar, inc=1, device_id=(lax.rem(v + h, W), o), device_id_type=MESH)

        c_occ.wait()
        c_sing.wait()
        for j in range(NJ):
            amps[o, j] = sloc[j * GR:(j + 1) * GR, :]
        for q in range(Q):
            for j in range(NJ):
                gath[o, q * NJ + j] = oloc[q, j * GR:(j + 1) * GR, 0:MAIN]
            rows[q * R:(q + 1) * R, 0:OCC] = oloc[q, :, 0:OCC]
        if TAIL:
            for g in range(GROUPS):
                parts = [oloc[min(g * SLOTS + t, Q - 1), :, MAIN:N] for t in range(SLOTS)]
                packed = jnp.concatenate(parts, axis=1) if SLOTS > 1 else parts[0]
                for j in range(NJ):
                    tails[o, g * NJ + j, :, 0:SLOTS * TAIL] = packed[j * GR:(j + 1) * GR]
        ri = lax.broadcasted_iota(jnp.int32, (R, KP), 0) + o * R
        ci = lax.broadcasted_iota(jnp.int32, (R, KP), 1)
        mask = ri == ci
        lane = lax.broadcasted_iota(jnp.int32, (GR, LANES), 1)
        tr = jnp.zeros((GR, LANES), F32)
        for q in range(Q):
            dq = jnp.sum(jnp.where(mask, oloc[q, :, 0:KP], 0.0), axis=0, keepdims=True)
            tq = jnp.sum(dq, axis=1, keepdims=True)
            tr = tr + jnp.where(lane == q, jnp.broadcast_to(tq, (GR, LANES)), 0.0)
        tails[o, GROUPS * NJ] = tr

        pl.semaphore_wait(bar, has_r.astype(jnp.int32) + has_l.astype(jnp.int32) + W)

        def piece(d, u):
            if isinstance(u, str):
                return {"a": amps, "t": tails}[u].at[d], {"a": Q, "t": Q + 1}[u]
            return gath.at[d, pl.ds(u * NJ, NJ)], u

        def remote(d, u, sems, target):
            ref, i = piece(d, u)
            return pltpu.make_async_remote_copy(
                src_ref=ref, dst_ref=ref, send_sem=sems.at[d, i], recv_sem=r_sem.at[d, i],
                device_id=(v, target), device_id_type=MESH)

        def send_own(u):
            @pl.when(has_r)
            def _():
                remote(o, u, s_right, right).start()

            @pl.when(has_l)
            def _():
                remote(o, u, s_left, left).start()

            remote(o, u, s_part, part).start()

        def relay(u):
            for h in range(1, NZ):
                @pl.when(z - h >= 0)
                def _():
                    d = (z - h) * CORES + k
                    remote(d, u, s_right, right).wait_recv()

                    @pl.when(has_r)
                    def _():
                        remote(d, u, s_right, right).start()

                    remote(d, u, s_part, part).start()

                @pl.when(z + h < NZ)
                def _():
                    d = (z + h) * CORES + k
                    remote(d, u, s_left, left).wait_recv()

                    @pl.when(has_l)
                    def _():
                        remote(d, u, s_left, left).start()

                    remote(d, u, s_part, part).start()

            for s in range(NZ):
                remote(s * CORES + 1 - k, u, s_part, part).wait_recv()

        def finish(u):
            for s in range(NZ):
                d = s * CORES + k

                @pl.when(jnp.logical_and(s <= z, has_r))
                def _():
                    remote(d, u, s_right, right).wait_send()

                @pl.when(jnp.logical_and(s >= z, has_l))
                def _():
                    remote(d, u, s_left, left).wait_send()

                remote(d, u, s_part, part).wait_send()

        send_own("a")
        send_own("t")

        @pl.loop(0, Q)
        def _(u):
            send_own(u)

        relay("a")
        relay("t")

        for d in range(D):
            for j in range(NJ):
                at = d * R + j * GR
                xbuf[at:at + GR, 0:A] = amps[d, j]
        amp = xbuf[:, 0:A]
        tmat[...] = jnp.zeros_like(tmat)
        shifted = jnp.concatenate([jnp.zeros((OCC, OCC), F32), amp], axis=1)
        thi, tlo = split(shifted)
        tmat[0:OCC, :] = thi
        tmat[KP:KP + OCC, :] = tlo
        ahi, alo = split(amp)
        pick = (lax.broadcasted_iota(jnp.int32, (RV, A), 1)
                == lax.broadcasted_iota(jnp.int32, (RV, A), 0) + o * RV)
        pick = jnp.where(pick, 1.0, 0.0).astype(BF16)

        def take(x):
            return lax.dot_general(pick, x, (((1,), (1,)), ((), ())), preferred_element_type=F32)

        sleft[0, :, 0:OCC] = take(ahi).astype(BF16)
        sleft[1, :, 0:OCC] = take(alo).astype(BF16)

        def dress(x):
            hi, lo = split(x)
            return dot(jnp.concatenate([hi, hi], axis=1), tmat[...]) + dot(lo, tmat[0:KP, :])

        keep = lax.broadcasted_iota(jnp.int32, (ROWS, KP), 1) < OCC
        extra = dress(jnp.where(keep, rows[...], 0.0))
        for q in range(Q):
            drows[q * R:(q + 1) * R, :] = oloc[q] + extra[q * R:(q + 1) * R]
        for w in range(W):
            sl = drows[:, OCC + w * PIECE:OCC + (w + 1) * PIECE]
            for g in range(GRAN):
                ovsend[w, g] = sl[g * GR:(g + 1) * GR]
        total = tails[0, GROUPS * NJ]
        for d in range(1, D):
            total = total + tails[d, GROUPS * NJ]
        fock = jnp.zeros((R, N), F32)
        for q in range(Q):
            fock = fock + total[0:1, q:q + 1] * drows[q * R:(q + 1) * R, :]
        fock = fock[:, OCC:]
        for j in range(NJ):
            fbuf[v, j] = fock[j * GR:(j + 1) * GR]

        def ov_copy(h):
            w = lax.rem(v + h, W)
            return pltpu.make_async_remote_copy(
                src_ref=ovsend.at[w], dst_ref=ovrecv.at[v], send_sem=ov_s.at[h],
                recv_sem=ov_r.at[h], device_id=(w, o), device_id_type=MESH)

        def f_copy(h):
            w = lax.rem(v + h, W)
            return pltpu.make_async_remote_copy(
                src_ref=fbuf.at[v], dst_ref=fbuf.at[v], send_sem=f_s.at[h],
                recv_sem=f_r.at[h], device_id=(w, o), device_id_type=MESH)

        for h in range(1, W):
            ov_copy(h).start()
            f_copy(h).start()
        ovrecv[v] = ovsend[v]

        shi = sleft[0, :, 0:OCC]
        slo = sleft[1, :, 0:OCC]

        @pl.loop(0, Q)
        def _(q):
            relay(q)
            if TAIL:
                shift = lax.rem(LANES - lax.rem(q, SLOTS) * TAIL, LANES)
            for d in range(D):
                for j in range(NJ):
                    at = d * R + j * GR
                    xbuf[at:at + GR, 0:MAIN] = gath[d, q * NJ + j]
                    if TAIL:
                        t = pltpu.roll(tails[d, (q // SLOTS) * NJ + j], shift, axis=1)
                        xbuf[at:at + GR, MAIN:N] = t[:, 0:TAIL]
            hi, lo = split(xbuf[...])
            prod = dot(shi, hi) + (dot(shi, lo) + dot(slo, hi))
            vin(q).wait()
            vloc[q] = vloc[q] - prod
            keep_v = lax.broadcasted_iota(jnp.int32, (RV, KP), 1) < OCC
            vloc[q] = vloc[q] + dress(jnp.where(keep_v, vloc[q, :, 0:KP], 0.0))
            vout(q).start()

        for h in range(1, W):
            ov_copy(h).wait_recv()
            f_copy(h).wait_recv()
        for w in range(W):
            for g in range(GRAN):
                j = g % NJ
                ovout[w * Q + g // NJ, j * GR:(j + 1) * GR, :] = ovrecv[w, g]
        c_ov = pltpu.make_async_copy(ovout, out_ov, o_out.at[0])
        c_ov.start()
        for j in range(NJ):
            acc = fbuf[0, j]
            for w in range(1, W):
                acc = acc + fbuf[w, j]
            fout[j * GR:(j + 1) * GR, :] = acc / (Q * W)
        c_f = pltpu.make_async_copy(fout, out_fock, o_out.at[1])
        c_f.start()

        finish("a")
        finish("t")

        @pl.loop(0, Q)
        def _(u):
            finish(u)
            vout(u).wait()

        for h in range(1, W):
            ov_copy(h).wait_send()
            f_copy(h).wait_send()
        c_ov.wait()
        c_f.wait()

    DMA = pltpu.SemaphoreType.DMA
    V = pltpu.VMEM
    any_spec = pl.BlockSpec(memory_space=pl.ANY)
    return pl.pallas_call(
        kernel,
        name="dress",
        out_shape=(jax.ShapeDtypeStruct((Q, RV, N), F32),
                   jax.ShapeDtypeStruct((Q * W, R, PIECE), F32),
                   jax.ShapeDtypeStruct((R, A), F32)),
        in_specs=[any_spec] * 3,
        out_specs=(any_spec,) * 3,
        scratch_shapes=[
            V((D, GRAN, GR, MAIN), F32),
            V((D, NJ, GR, A), F32),
            V((D, GROUPS * NJ + 1, GR, LANES), F32),
            V((Q, RV, N), F32),
            V((Q, R, N), F32),
            V((R, A), F32),
            V((OCC, N), F32),
            V((ROWS, KP), F32),
            V((ROWS, N), F32),
            V((2 * KP, N), BF16),
            V((2, RV, KP), BF16),
            V((W, GRAN, GR, PIECE), F32),
            V((W, GRAN, GR, PIECE), F32),
            V((Q * W, R, PIECE), F32),
            V((W, NJ, GR, A), F32),
            V((R, A), F32),
            DMA((D, UNITS)), DMA((D, UNITS)), DMA((D, UNITS)), DMA((D, UNITS)),
            DMA((W,)), DMA((W,)), DMA((W,)), DMA((W,)),
            DMA((2,)), DMA((Q,)), DMA((Q,)), DMA((2,)),
        ],
        compiler_params=pltpu.CompilerParams(
            collective_id=0, has_side_effects=True, vmem_limit_bytes=40 * 2**20),
    )


def solution(mesh):
    W, D = mesh.shape["vec"], mesh.shape["orb"]

    def shards(chol_occ, chol_vir, singles):
        Q, R, N = chol_occ.shape
        call = make_kernel(W, D, Q, R, chol_vir.shape[1], N, singles.shape[1])
        return call(chol_occ, chol_vir, singles)

    return jax.shard_map(
        shards,
        mesh=mesh,
        in_specs=(P("vec", "orb", None), P("vec", "orb", None), P("orb", None)),
        out_specs=(P("vec", "orb", None), P(None, "orb", "vec"), P("orb", None)),
        check_vma=False,
    )
```

```python
import jax
import jax.numpy as jnp
from jax import lax
from jax.experimental import pallas as pl
from jax.experimental.pallas import tpu as pltpu
from jax.sharding import PartitionSpec as P

MESH = pl.DeviceIdType.MESH
F32, BF16 = jnp.float32, jnp.bfloat16
LANES = 128
CORES = 2


def split(x):
    hi = x.astype(BF16)
    return hi, (x - hi.astype(F32)).astype(BF16)


def dot(a, b):
    return jnp.dot(a, b, preferred_element_type=F32)


def make_kernel(W, D, Q, R, RV, N, A):
    OCC = N - A
    NZ = D // CORES
    GR = 8 if R % 8 == 0 else (4 if R % 4 == 0 else R)
    NJ = R // GR
    ROWS = Q * R
    GRAN = Q * NJ
    MAIN = N // LANES * LANES
    TAIL = N - MAIN
    SLOTS = LANES // TAIL if TAIL else 1
    GROUPS = -(-Q // SLOTS)
    PIECE = A // W
    KP = -(-OCC // LANES) * LANES
    UNITS = Q + 2
    NP = -(-N // LANES) * LANES
    AP = -(-A // LANES) * LANES
    VP = -(-RV // LANES) * LANES

    def kernel(occ, vir, sing, out_vir, out_ov, out_fock,
               gath, amps, tails, vloc, oloc, sloc, xbuf, drows, tmat, tright, sleft, lwts,
               ovsend, ovrecv, ovout, fbuf, fout,
               s_right, s_left, s_part, r_sem, ov_s, ov_r, f_s, f_r, in_sem, v_in, v_out, o_out):
        v = lax.axis_index("vec")
        o = lax.axis_index("orb")
        z = o // CORES
        k = o % CORES
        has_r = z < NZ - 1
        has_l = z > 0
        right = lax.rem(o + CORES, D)
        left = lax.rem(o - CORES + D, D)
        part = z * CORES + (1 - k)

        c_occ = pltpu.make_async_copy(occ, oloc, in_sem.at[0])
        c_sing = pltpu.make_async_copy(sing, sloc, in_sem.at[1])
        c_occ.start()
        c_sing.start()

        def vin(q):
            return pltpu.make_async_copy(vir.at[q], vloc.at[q], v_in.at[q])

        def vout(q):
            return pltpu.make_async_copy(vloc.at[q], out_vir.at[q], v_out.at[q])

        @pl.loop(0, Q)
        def _(q):
            vin(q).start()

        bar = pltpu.get_barrier_semaphore()

        @pl.when(has_r)
        def _():
            pl.semaphore_signal(bar, inc=1, device_id=(v, right), device_id_type=MESH)

        @pl.when(has_l)
        def _():
            pl.semaphore_signal(bar, inc=1, device_id=(v, left), device_id_type=MESH)

        pl.semaphore_signal(bar, inc=1, device_id=(v, part), device_id_type=MESH)
        for h in range(1, W):
            pl.semaphore_signal(bar, inc=1, device_id=(lax.rem(v + h, W), o), device_id_type=MESH)

        c_occ.wait()
        c_sing.wait()
        for j in range(NJ):
            amps[o, j] = sloc[j * GR:(j + 1) * GR, :]
        for q in range(Q):
            for j in range(NJ):
                gath[o, q * NJ + j] = oloc[q, j * GR:(j + 1) * GR, 0:MAIN]
        if TAIL:
            for g in range(GROUPS):
                parts = [oloc[min(g * SLOTS + t, Q - 1), :, MAIN:N] for t in range(SLOTS)]
                packed = jnp.concatenate(parts, axis=1) if SLOTS > 1 else parts[0]
                for j in range(NJ):
                    tails[o, g * NJ + j, :, 0:SLOTS * TAIL] = packed[j * GR:(j + 1) * GR]
        ri = lax.broadcasted_iota(jnp.int32, (R, KP), 0) + o * R
        ci = lax.broadcasted_iota(jnp.int32, (R, KP), 1)
        mask = ri == ci
        lane = lax.broadcasted_iota(jnp.int32, (GR, LANES), 1)
        tr = jnp.zeros((GR, LANES), F32)
        for q in range(Q):
            dq = jnp.sum(jnp.where(mask, oloc[q, :, 0:KP], 0.0), axis=0, keepdims=True)
            tq = jnp.sum(dq, axis=1, keepdims=True)
            tr = tr + jnp.where(lane == q, jnp.broadcast_to(tq, (GR, LANES)), 0.0)
        tails[o, GROUPS * NJ] = tr

        pl.semaphore_wait(bar, has_r.astype(jnp.int32) + has_l.astype(jnp.int32) + W)

        def piece(d, u):
            if isinstance(u, str):
                return {"a": amps, "t": tails}[u].at[d], {"a": Q, "t": Q + 1}[u]
            return gath.at[d, pl.ds(u * NJ, NJ)], u

        def remote(d, u, sems, target):
            ref, i = piece(d, u)
            return pltpu.make_async_remote_copy(
                src_ref=ref, dst_ref=ref, send_sem=sems.at[d, i], recv_sem=r_sem.at[d, i],
                device_id=(v, target), device_id_type=MESH)

        def send_own(u):
            @pl.when(has_r)
            def _():
                remote(o, u, s_right, right).start()

            @pl.when(has_l)
            def _():
                remote(o, u, s_left, left).start()

            remote(o, u, s_part, part).start()

        def relay(u):
            for h in range(1, NZ):
                @pl.when(z - h >= 0)
                def _():
                    d = (z - h) * CORES + k
                    remote(d, u, s_right, right).wait_recv()

                    @pl.when(has_r)
                    def _():
                        remote(d, u, s_right, right).start()

                    remote(d, u, s_part, part).start()

                @pl.when(z + h < NZ)
                def _():
                    d = (z + h) * CORES + k
                    remote(d, u, s_left, left).wait_recv()

                    @pl.when(has_l)
                    def _():
                        remote(d, u, s_left, left).start()

                    remote(d, u, s_part, part).start()

            for s in range(NZ):
                remote(s * CORES + 1 - k, u, s_part, part).wait_recv()

        def finish(u):
            for s in range(NZ):
                d = s * CORES + k

                @pl.when(jnp.logical_and(s <= z, has_r))
                def _():
                    remote(d, u, s_right, right).wait_send()

                @pl.when(jnp.logical_and(s >= z, has_l))
                def _():
                    remote(d, u, s_left, left).wait_send()

                remote(d, u, s_part, part).wait_send()

        send_own("a")
        send_own("t")

        @pl.loop(0, Q)
        def _(u):
            send_own(u)

        relay("a")
        relay("t")

        xbuf[...] = jnp.zeros_like(xbuf)
        for d in range(D):
            for j in range(NJ):
                at = d * R + j * GR
                xbuf[at:at + GR, 0:A] = amps[d, j]
        amp = xbuf[0:OCC, 0:A]
        tmat[...] = jnp.zeros_like(tmat)
        shifted = jnp.concatenate([jnp.zeros((OCC, OCC), F32), amp], axis=1)
        thi, tlo = split(shifted)
        tmat[0:OCC, :] = thi
        tmat[KP:KP + OCC, :] = tlo
        thi, tlo = split(jnp.transpose(xbuf[:, 0:AP])[0:A])
        tright[:, 0:KP] = thi
        tright[:, KP:2 * KP] = tlo
        ahi, alo = split(xbuf[:, 0:A])
        pick = (lax.broadcasted_iota(jnp.int32, (A, VP), 0)
                == lax.broadcasted_iota(jnp.int32, (A, VP), 1) + o * RV)
        pick = jnp.where(pick, 1.0, 0.0).astype(BF16)
        shi = dot(ahi, pick).astype(BF16)
        sleft[0:KP, 0:VP] = shi
        sleft[KP:2 * KP, 0:VP] = shi
        sleft[0:KP, VP:2 * VP] = dot(alo, pick).astype(BF16)
        sleft[KP:2 * KP, VP:2 * VP] = jnp.zeros((KP, VP), BF16)
        lwts[...] = jnp.zeros_like(lwts)

        for q in range(Q):
            for r in range(R):
                drows[r * Q + q:r * Q + q + 1, :] = oloc[q, r:r + 1, :]
        keep = lax.broadcasted_iota(jnp.int32, (ROWS, KP), 1) < OCC
        hi, lo = split(jnp.where(keep, drows[:, 0:KP], 0.0))
        extra = dot(jnp.concatenate([hi, hi], axis=1), tmat[...]) + dot(lo, tmat[0:KP, :])
        drows[...] = drows[...] + extra
        for w in range(W):
            sl = drows[:, OCC + w * PIECE:OCC + (w + 1) * PIECE]
            for r in range(R):
                ovsend[w, r] = sl[r * Q:(r + 1) * Q]
        total = tails[0, GROUPS * NJ]
        for d in range(1, D):
            total = total + tails[d, GROUPS * NJ]
        rid = lax.broadcasted_iota(jnp.int32, (R, ROWS), 0) * Q
        cid = lax.broadcasted_iota(jnp.int32, (R, ROWS), 1)
        wts = jnp.zeros((R, ROWS), F32)
        for q in range(Q):
            wts = wts + jnp.where(cid == rid + q, jnp.broadcast_to(total[0:1, q:q + 1], (R, ROWS)), 0.0)
        whi, wlo = split(wts)
        dhi, dlo = split(drows[...])
        fock = (dot(whi, dhi) + (dot(whi, dlo) + dot(wlo, dhi)))[:, OCC:]
        for j in range(NJ):
            fbuf[v, j] = fock[j * GR:(j + 1) * GR]

        def ov_copy(h):
            w = lax.rem(v + h, W)
            return pltpu.make_async_remote_copy(
                src_ref=ovsend.at[w], dst_ref=ovrecv.at[v], send_sem=ov_s.at[h],
                recv_sem=ov_r.at[h], device_id=(w, o), device_id_type=MESH)

        def f_copy(h):
            w = lax.rem(v + h, W)
            return pltpu.make_async_remote_copy(
                src_ref=fbuf.at[v], dst_ref=fbuf.at[v], send_sem=f_s.at[h],
                recv_sem=f_r.at[h], device_id=(w, o), device_id_type=MESH)

        for h in range(1, W):
            ov_copy(h).start()
            f_copy(h).start()
        ovrecv[v] = ovsend[v]

        @pl.loop(0, Q)
        def _(q):
            relay(q)
            if TAIL:
                shift = lax.rem(LANES - lax.rem(q, SLOTS) * TAIL, LANES)
            for d in range(D):
                for j in range(NJ):
                    at = d * R + j * GR
                    xbuf[at:at + GR, 0:MAIN] = gath[d, q * NJ + j]
                    if TAIL:
                        t = pltpu.roll(tails[d, (q // SLOTS) * NJ + j], shift, axis=1)
                        xbuf[at:at + GR, MAIN:N] = t[:, 0:TAIL]
            hi, lo = split(jnp.transpose(xbuf[...])[0:N])
            prod = dot(jnp.concatenate([hi, lo], axis=1), sleft[...])
            prod = prod[:, 0:VP] + prod[:, VP:2 * VP]
            vin(q).wait()
            vloc[q] = vloc[q] - prod[:, 0:RV]
            hi, lo = split(vloc[q, 0:OCC, :])
            lwts[0:OCC, 0:RV] = hi
            lwts[KP:KP + OCC, 0:RV] = hi
            lwts[0:OCC, VP:VP + RV] = lo
            prod = dot(tright[...], lwts[...])
            prod = prod[:, 0:VP] + prod[:, VP:2 * VP]
            vloc[q, OCC:N, :] = vloc[q, OCC:N, :] + prod[:, 0:RV]
            vout(q).start()

        for h in range(1, W):
            ov_copy(h).wait_recv()
            f_copy(h).wait_recv()
        for w in range(W):
            for r in range(R):
                ovout[r, w * Q:(w + 1) * Q, :] = ovrecv[w, r]
        c_ov = pltpu.make_async_copy(ovout, out_ov, o_out.at[0])
        c_ov.start()
        for j in range(NJ):
            acc = fbuf[0, j]
            for w in range(1, W):
                acc = acc + fbuf[w, j]
            fout[j * GR:(j + 1) * GR, :] = acc / (Q * W)
        c_f = pltpu.make_async_copy(fout, out_fock, o_out.at[1])
        c_f.start()

        finish("a")
        finish("t")

        @pl.loop(0, Q)
        def _(u):
            finish(u)
            vout(u).wait()

        for h in range(1, W):
            ov_copy(h).wait_send()
            f_copy(h).wait_send()
        c_ov.wait()
        c_f.wait()

    DMA = pltpu.SemaphoreType.DMA
    V = pltpu.VMEM
    any_spec = pl.BlockSpec(memory_space=pl.ANY)
    return pl.pallas_call(
        kernel,
        name="dress",
        out_shape=(jax.ShapeDtypeStruct((Q, N, RV), F32),
                   jax.ShapeDtypeStruct((R, Q * W, PIECE), F32),
                   jax.ShapeDtypeStruct((R, A), F32)),
        in_specs=[pl.BlockSpec(memory_space=pltpu.HBM)] * 3,
        out_specs=(any_spec,) * 3,
        scratch_shapes=[
            V((D, GRAN, GR, MAIN), F32),
            V((D, NJ, GR, A), F32),
            V((D, GROUPS * NJ + 1, GR, LANES), F32),
            V((Q, N, RV), F32),
            V((Q, R, N), F32),
            V((R, A), F32),
            V((KP, NP), F32),
            V((ROWS, N), F32),
            V((2 * KP, N), BF16),
            V((A, 2 * KP), BF16),
            V((2 * KP, 2 * VP), BF16),
            V((2 * KP, 2 * VP), BF16),
            V((W, R, Q, PIECE), F32),
            V((W, R, Q, PIECE), F32),
            V((R, Q * W, PIECE), F32),
            V((W, NJ, GR, A), F32),
            V((R, A), F32),
            DMA((D, UNITS)), DMA((D, UNITS)), DMA((D, UNITS)), DMA((D, UNITS)),
            DMA((W,)), DMA((W,)), DMA((W,)), DMA((W,)),
            DMA((2,)), DMA((Q,)), DMA((Q,)), DMA((2,)),
        ],
        compiler_params=pltpu.CompilerParams(
            collective_id=0, has_side_effects=True, vmem_limit_bytes=40 * 2**20),
    )


def solution(mesh):
    W, D = mesh.shape["vec"], mesh.shape["orb"]

    def shards(chol_occ, chol_vir, singles):
        Q, R, N = chol_occ.shape
        call = make_kernel(W, D, Q, R, chol_vir.shape[1], N, singles.shape[1])
        vir, ov, fock = call(chol_occ, jnp.swapaxes(chol_vir, 1, 2), singles)
        return jnp.swapaxes(vir, 1, 2), jnp.swapaxes(ov, 0, 1), fock

    return jax.shard_map(
        shards,
        mesh=mesh,
        in_specs=(P("vec", "orb", None), P("vec", "orb", None), P("orb", None)),
        out_specs=(P("vec", "orb", None), P(None, "orb", "vec"), P("orb", None)),
        check_vma=False,
    )
```

```python
import jax
import jax.numpy as jnp
from jax import lax
from jax.experimental import pallas as pl
from jax.experimental.pallas import tpu as pltpu
from jax.sharding import PartitionSpec as P

MESH = pl.DeviceIdType.MESH
F32, BF16 = jnp.float32, jnp.bfloat16
LANES = 128
CORES = 2
SKEW = 2
AHEAD = 4


def split(x):
    hi = x.astype(BF16)
    return hi, (x - hi.astype(F32)).astype(BF16)


def dot(a, b):
    return jnp.dot(a, b, preferred_element_type=F32)


def make_kernel(W, D, Q, R, RV, N, A):
    OCC = N - A
    NZ = D // CORES
    GR = 8 if R % 8 == 0 else (4 if R % 4 == 0 else R)
    NJ = R // GR
    ROWS = Q * R
    GRAN = Q * NJ
    MAIN = N // LANES * LANES
    TAIL = N - MAIN
    SLOTS = LANES // TAIL if TAIL else 1
    GROUPS = -(-Q // SLOTS)
    PIECE = A // W
    KP = -(-OCC // LANES) * LANES
    UNITS = Q + 2
    NP = -(-N // LANES) * LANES
    AP = -(-A // LANES) * LANES
    VP = -(-RV // LANES) * LANES

    def kernel(occ, vir, sing, out_vir, out_ov, out_fock,
               gath, amps, tails, vloc, oloc, sloc, xbuf, drows, tmat, tright, sleft, lwts,
               ovsend, ovrecv, ovout, fbuf, fout,
               s_right, s_left, s_part, r_sem, ov_s, ov_r, f_s, f_r, in_sem, v_in, v_out, o_out):
        v = lax.axis_index("vec")
        o = lax.axis_index("orb")
        z = o // CORES
        k = o % CORES
        has_r = z < NZ - 1
        has_l = z > 0
        right = lax.rem(o + CORES, D)
        left = lax.rem(o - CORES + D, D)
        part = z * CORES + (1 - k)

        c_occ = pltpu.make_async_copy(occ, oloc, in_sem.at[0])
        c_sing = pltpu.make_async_copy(sing, sloc, in_sem.at[1])
        c_occ.start()
        c_sing.start()

        def vin(q):
            return pltpu.make_async_copy(vir.at[q], vloc.at[q], v_in.at[q])

        def vout(q):
            return pltpu.make_async_copy(vloc.at[q], out_vir.at[q], v_out.at[q])

        @pl.loop(0, Q)
        def _(q):
            vin(q).start()

        bar = pltpu.get_barrier_semaphore()

        @pl.when(has_r)
        def _():
            pl.semaphore_signal(bar, inc=1, device_id=(v, right), device_id_type=MESH)

        @pl.when(has_l)
        def _():
            pl.semaphore_signal(bar, inc=1, device_id=(v, left), device_id_type=MESH)

        pl.semaphore_signal(bar, inc=1, device_id=(v, part), device_id_type=MESH)
        for h in range(1, W):
            pl.semaphore_signal(bar, inc=1, device_id=(lax.rem(v + h, W), o), device_id_type=MESH)

        c_occ.wait()
        c_sing.wait()
        for j in range(NJ):
            amps[o, j] = sloc[j * GR:(j + 1) * GR, :]
        for q in range(Q):
            for j in range(NJ):
                gath[o, q * NJ + j] = oloc[q, j * GR:(j + 1) * GR, 0:MAIN]
        if TAIL:
            for g in range(GROUPS):
                parts = [oloc[min(g * SLOTS + t, Q - 1), :, MAIN:N] for t in range(SLOTS)]
                packed = jnp.concatenate(parts, axis=1) if SLOTS > 1 else parts[0]
                for j in range(NJ):
                    tails[o, g * NJ + j, :, 0:SLOTS * TAIL] = packed[j * GR:(j + 1) * GR]
        ri = lax.broadcasted_iota(jnp.int32, (R, KP), 0) + o * R
        ci = lax.broadcasted_iota(jnp.int32, (R, KP), 1)
        mask = ri == ci
        lane = lax.broadcasted_iota(jnp.int32, (GR, LANES), 1)
        tr = jnp.zeros((GR, LANES), F32)
        for q in range(Q):
            dq = jnp.sum(jnp.where(mask, oloc[q, :, 0:KP], 0.0), axis=0, keepdims=True)
            tq = jnp.sum(dq, axis=1, keepdims=True)
            tr = tr + jnp.where(lane == q, jnp.broadcast_to(tq, (GR, LANES)), 0.0)
        tails[o, GROUPS * NJ] = tr

        pl.semaphore_wait(bar, has_r.astype(jnp.int32) + has_l.astype(jnp.int32) + W)

        def piece(d, u):
            if isinstance(u, str):
                return {"a": amps, "t": tails}[u].at[d], {"a": Q, "t": Q + 1}[u]
            return gath.at[d, pl.ds(u * NJ, NJ)], u

        def remote(d, u, sems, target):
            ref, i = piece(d, u)
            return pltpu.make_async_remote_copy(
                src_ref=ref, dst_ref=ref, send_sem=sems.at[d, i], recv_sem=r_sem.at[d, i],
                device_id=(v, target), device_id_type=MESH)

        def send_own(u):
            @pl.when(has_r)
            def _():
                remote(o, u, s_right, right).start()

            @pl.when(has_l)
            def _():
                remote(o, u, s_left, left).start()

            remote(o, u, s_part, part).start()

        def relay(h, u):
            @pl.when(z - h >= 0)
            def _():
                d = (z - h) * CORES + k
                remote(d, u, s_right, right).wait_recv()

                @pl.when(has_r)
                def _():
                    remote(d, u, s_right, right).start()

                remote(d, u, s_part, part).start()

            @pl.when(z + h < NZ)
            def _():
                d = (z + h) * CORES + k
                remote(d, u, s_left, left).wait_recv()

                @pl.when(has_l)
                def _():
                    remote(d, u, s_left, left).start()

                remote(d, u, s_part, part).start()

        def from_partner(u):
            for s in range(NZ):
                remote(s * CORES + 1 - k, u, s_part, part).wait_recv()

        units = ["a", "t"] + list(range(Q))
        LEAD = 2 + SKEW * max(NZ - 2, 0)

        def finish(u):
            for s in range(NZ):
                d = s * CORES + k

                @pl.when(jnp.logical_and(s <= z, has_r))
                def _():
                    remote(d, u, s_right, right).wait_send()

                @pl.when(jnp.logical_and(s >= z, has_l))
                def _():
                    remote(d, u, s_left, left).wait_send()

                remote(d, u, s_part, part).wait_send()

        for u in units[:AHEAD]:
            send_own(u)

        for q in range(Q):
            for r in range(R):
                drows[r * Q + q:r * Q + q + 1, :] = oloc[q, r:r + 1, :]

        for t in range(LEAD):
            if AHEAD <= t + AHEAD < UNITS:
                send_own(units[t + AHEAD])
            for h in range(1, NZ):
                n = t - SKEW * (h - 1)
                if 0 <= n < UNITS:
                    relay(h, units[n])
        from_partner("a")
        from_partner("t")

        xbuf[...] = jnp.zeros_like(xbuf)
        for d in range(D):
            for j in range(NJ):
                at = d * R + j * GR
                xbuf[at:at + GR, 0:A] = amps[d, j]
        amp = xbuf[0:OCC, 0:A]
        tmat[...] = jnp.zeros_like(tmat)
        shifted = jnp.concatenate([jnp.zeros((OCC, OCC), F32), amp], axis=1)
        thi, tlo = split(shifted)
        tmat[0:OCC, :] = thi
        tmat[KP:KP + OCC, :] = tlo
        thi, tlo = split(jnp.transpose(xbuf[:, 0:AP])[0:A])
        tright[:, 0:KP] = thi
        tright[:, KP:2 * KP] = tlo
        ahi, alo = split(xbuf[:, 0:A])
        pick = (lax.broadcasted_iota(jnp.int32, (A, VP), 0)
                == lax.broadcasted_iota(jnp.int32, (A, VP), 1) + o * RV)
        pick = jnp.where(pick, 1.0, 0.0).astype(BF16)
        shi = dot(ahi, pick).astype(BF16)
        sleft[0:KP, 0:VP] = shi
        sleft[KP:2 * KP, 0:VP] = shi
        sleft[0:KP, VP:2 * VP] = dot(alo, pick).astype(BF16)
        sleft[KP:2 * KP, VP:2 * VP] = jnp.zeros((KP, VP), BF16)
        lwts[...] = jnp.zeros_like(lwts)

        keep = lax.broadcasted_iota(jnp.int32, (ROWS, KP), 1) < OCC
        hi, lo = split(jnp.where(keep, drows[:, 0:KP], 0.0))
        extra = dot(jnp.concatenate([hi, hi], axis=1), tmat[...]) + dot(lo, tmat[0:KP, :])
        drows[...] = drows[...] + extra
        for w in range(W):
            sl = drows[:, OCC + w * PIECE:OCC + (w + 1) * PIECE]
            for r in range(R):
                ovsend[w, r] = sl[r * Q:(r + 1) * Q]
        total = tails[0, GROUPS * NJ]
        for d in range(1, D):
            total = total + tails[d, GROUPS * NJ]
        rid = lax.broadcasted_iota(jnp.int32, (R, ROWS), 0) * Q
        cid = lax.broadcasted_iota(jnp.int32, (R, ROWS), 1)
        wts = jnp.zeros((R, ROWS), F32)
        for q in range(Q):
            wts = wts + jnp.where(cid == rid + q, jnp.broadcast_to(total[0:1, q:q + 1], (R, ROWS)), 0.0)
        whi, wlo = split(wts)
        dhi, dlo = split(drows[...])
        fock = (dot(whi, dhi) + (dot(whi, dlo) + dot(wlo, dhi)))[:, OCC:]
        for j in range(NJ):
            fbuf[v, j] = fock[j * GR:(j + 1) * GR]

        def ov_copy(h):
            w = lax.rem(v + h, W)
            return pltpu.make_async_remote_copy(
                src_ref=ovsend.at[w], dst_ref=ovrecv.at[v], send_sem=ov_s.at[h],
                recv_sem=ov_r.at[h], device_id=(w, o), device_id_type=MESH)

        def f_copy(h):
            w = lax.rem(v + h, W)
            return pltpu.make_async_remote_copy(
                src_ref=fbuf.at[v], dst_ref=fbuf.at[v], send_sem=f_s.at[h],
                recv_sem=f_r.at[h], device_id=(w, o), device_id_type=MESH)

        for h in range(1, W):
            ov_copy(h).start()
            f_copy(h).start()
        ovrecv[v] = ovsend[v]

        @pl.loop(0, Q)
        def _(q):
            @pl.when(q + LEAD + AHEAD < UNITS)
            def _():
                send_own(q + LEAD + AHEAD - 2)

            for h in range(1, NZ):
                n = q + LEAD - SKEW * (h - 1)

                @pl.when(n < UNITS)
                def _():
                    relay(h, n - 2)

            from_partner(q)
            if TAIL:
                shift = lax.rem(LANES - lax.rem(q, SLOTS) * TAIL, LANES)
            for d in range(D):
                for j in range(NJ):
                    at = d * R + j * GR
                    xbuf[at:at + GR, 0:MAIN] = gath[d, q * NJ + j]
                    if TAIL:
                        t = pltpu.roll(tails[d, (q // SLOTS) * NJ + j], shift, axis=1)
                        xbuf[at:at + GR, MAIN:N] = t[:, 0:TAIL]
            hi, lo = split(jnp.transpose(xbuf[...])[0:N])
            prod = dot(jnp.concatenate([hi, lo], axis=1), sleft[...])
            prod = prod[:, 0:VP] + prod[:, VP:2 * VP]
            vin(q).wait()
            vloc[q] = vloc[q] - prod[:, 0:RV]
            hi, lo = split(vloc[q, 0:OCC, :])
            lwts[0:OCC, 0:RV] = hi
            lwts[KP:KP + OCC, 0:RV] = hi
            lwts[0:OCC, VP:VP + RV] = lo
            prod = dot(tright[...], lwts[...])
            prod = prod[:, 0:VP] + prod[:, VP:2 * VP]
            vloc[q, OCC:N, :] = vloc[q, OCC:N, :] + prod[:, 0:RV]
            vout(q).start()

        for h in range(1, W):
            ov_copy(h).wait_recv()
            f_copy(h).wait_recv()
        for w in range(W):
            for r in range(R):
                ovout[r, w * Q:(w + 1) * Q, :] = ovrecv[w, r]
        c_ov = pltpu.make_async_copy(ovout, out_ov, o_out.at[0])
        c_ov.start()
        for j in range(NJ):
            acc = fbuf[0, j]
            for w in range(1, W):
                acc = acc + fbuf[w, j]
            fout[j * GR:(j + 1) * GR, :] = acc / (Q * W)
        c_f = pltpu.make_async_copy(fout, out_fock, o_out.at[1])
        c_f.start()

        finish("a")
        finish("t")

        @pl.loop(0, Q)
        def _(u):
            finish(u)
            vout(u).wait()

        for h in range(1, W):
            ov_copy(h).wait_send()
            f_copy(h).wait_send()
        c_ov.wait()
        c_f.wait()

    DMA = pltpu.SemaphoreType.DMA
    V = pltpu.VMEM
    any_spec = pl.BlockSpec(memory_space=pl.ANY)
    return pl.pallas_call(
        kernel,
        name="dress",
        out_shape=(jax.ShapeDtypeStruct((Q, N, RV), F32),
                   jax.ShapeDtypeStruct((R, Q * W, PIECE), F32),
                   jax.ShapeDtypeStruct((R, A), F32)),
        in_specs=[pl.BlockSpec(memory_space=pltpu.HBM)] * 3,
        out_specs=(any_spec,) * 3,
        scratch_shapes=[
            V((D, GRAN, GR, MAIN), F32),
            V((D, NJ, GR, A), F32),
            V((D, GROUPS * NJ + 1, GR, LANES), F32),
            V((Q, N, RV), F32),
            V((Q, R, N), F32),
            V((R, A), F32),
            V((KP, NP), F32),
            V((ROWS, N), F32),
            V((2 * KP, N), BF16),
            V((A, 2 * KP), BF16),
            V((2 * KP, 2 * VP), BF16),
            V((2 * KP, 2 * VP), BF16),
            V((W, R, Q, PIECE), F32),
            V((W, R, Q, PIECE), F32),
            V((R, Q * W, PIECE), F32),
            V((W, NJ, GR, A), F32),
            V((R, A), F32),
            DMA((D, UNITS)), DMA((D, UNITS)), DMA((D, UNITS)), DMA((D, UNITS)),
            DMA((W,)), DMA((W,)), DMA((W,)), DMA((W,)),
            DMA((2,)), DMA((Q,)), DMA((Q,)), DMA((2,)),
        ],
        compiler_params=pltpu.CompilerParams(
            collective_id=0, has_side_effects=True, vmem_limit_bytes=40 * 2**20),
    )


def solution(mesh):
    W, D = mesh.shape["vec"], mesh.shape["orb"]

    def shards(chol_occ, chol_vir, singles):
        Q, R, N = chol_occ.shape
        call = make_kernel(W, D, Q, R, chol_vir.shape[1], N, singles.shape[1])
        args = (chol_occ, jnp.swapaxes(chol_vir, 1, 2), singles)
        vir, ov, fock = call(*(pltpu.with_memory_space_constraint(a, pltpu.HBM) for a in args))
        return jnp.swapaxes(vir, 1, 2), jnp.swapaxes(ov, 0, 1), fock

    return jax.shard_map(
        shards,
        mesh=mesh,
        in_specs=(P("vec", "orb", None), P("vec", "orb", None), P("orb", None)),
        out_specs=(P("vec", "orb", None), P(None, "orb", "vec"), P("orb", None)),
        check_vma=False,
    )
```

```python
import jax
import jax.numpy as jnp
from jax import lax
from jax.experimental import pallas as pl
from jax.experimental.pallas import tpu as pltpu
from jax.sharding import PartitionSpec as P

MESH = pl.DeviceIdType.MESH
F32, BF16 = jnp.float32, jnp.bfloat16
LANES = 128
CORES = 2
SKEW = 1
AHEAD = 5


def split(x):
    hi = x.astype(BF16)
    return hi, (x - hi.astype(F32)).astype(BF16)


def dot(a, b):
    return jnp.dot(a, b, preferred_element_type=F32)


def make_kernel(W, D, Q, R, RV, N, A):
    OCC = N - A
    NZ = D // CORES
    GR = 8 if R % 8 == 0 else (4 if R % 4 == 0 else R)
    NJ = R // GR
    ROWS = Q * R
    GRAN = Q * NJ
    MAIN = N // LANES * LANES
    TAIL = N - MAIN
    SLOTS = LANES // TAIL if TAIL else 1
    GROUPS = -(-Q // SLOTS)
    PIECE = A // W
    KP = -(-OCC // LANES) * LANES
    UNITS = Q + 2
    NP = -(-N // LANES) * LANES
    AP = -(-A // LANES) * LANES
    VP = -(-RV // LANES) * LANES

    def kernel(occ, vir, sing, out_vir, out_ov, out_fock,
               gath, amps, tails, vloc, oloc, sloc, xbuf, drows, tmat, tright, sleft, lwts,
               ovsend, ovrecv, ovout, fbuf, fout,
               s_right, s_left, s_part, r_sem, a_s, a_r, ov_s, ov_r, f_s, f_r, in_sem, v_in, v_out, o_out):
        v = lax.axis_index("vec")
        o = lax.axis_index("orb")
        z = o // CORES
        k = o % CORES
        has_r = z < NZ - 1
        has_l = z > 0
        right = lax.rem(o + CORES, D)
        left = lax.rem(o - CORES + D, D)
        part = z * CORES + (1 - k)

        c_occ = pltpu.make_async_copy(occ, oloc, in_sem.at[0])
        c_sing = pltpu.make_async_copy(sing, sloc, in_sem.at[1])
        c_occ.start()
        c_sing.start()

        def vin(q):
            return pltpu.make_async_copy(vir.at[q], vloc.at[q], v_in.at[q])

        def vout(q):
            return pltpu.make_async_copy(vloc.at[q], out_vir.at[q], v_out.at[q])

        bar = pltpu.get_barrier_semaphore()

        @pl.when(has_r)
        def _():
            pl.semaphore_signal(bar, inc=1, device_id=(v, right), device_id_type=MESH)

        @pl.when(has_l)
        def _():
            pl.semaphore_signal(bar, inc=1, device_id=(v, left), device_id_type=MESH)

        pl.semaphore_signal(bar, inc=1, device_id=(v, part), device_id_type=MESH)
        for h in range(1, W):
            pl.semaphore_signal(bar, inc=1, device_id=(lax.rem(v + h, W), o), device_id_type=MESH)

        c_occ.wait()
        c_sing.wait()
        for w in range(W):
            @pl.when(v == w)
            def _():
                cols = sloc[:, w * PIECE:(w + 1) * PIECE]
                for j in range(NJ):
                    amps[w, o, j] = cols[j * GR:(j + 1) * GR]
        for q in range(Q):
            for j in range(NJ):
                gath[o, q * NJ + j] = oloc[q, j * GR:(j + 1) * GR, 0:MAIN]
        if TAIL:
            for g in range(GROUPS):
                parts = [oloc[min(g * SLOTS + t, Q - 1), :, MAIN:N] for t in range(SLOTS)]
                packed = jnp.concatenate(parts, axis=1) if SLOTS > 1 else parts[0]
                for j in range(NJ):
                    tails[o, g * NJ + j, :, 0:SLOTS * TAIL] = packed[j * GR:(j + 1) * GR]
        ri = lax.broadcasted_iota(jnp.int32, (R, KP), 0) + o * R
        ci = lax.broadcasted_iota(jnp.int32, (R, KP), 1)
        mask = ri == ci
        lane = lax.broadcasted_iota(jnp.int32, (GR, LANES), 1)
        tr = jnp.zeros((GR, LANES), F32)
        for q in range(Q):
            dq = jnp.sum(jnp.where(mask, oloc[q, :, 0:KP], 0.0), axis=0, keepdims=True)
            tq = jnp.sum(dq, axis=1, keepdims=True)
            tr = tr + jnp.where(lane == q, jnp.broadcast_to(tq, (GR, LANES)), 0.0)
        tails[o, GROUPS * NJ] = tr

        pl.semaphore_wait(bar, has_r.astype(jnp.int32) + has_l.astype(jnp.int32) + W)

        def piece(d, u):
            if isinstance(u, str):
                return (amps.at[v, d], Q) if u == "a" else (tails.at[d], Q + 1)
            return gath.at[d, pl.ds(u * NJ, NJ)], u

        def remote(d, u, sems, target):
            ref, i = piece(d, u)
            return pltpu.make_async_remote_copy(
                src_ref=ref, dst_ref=ref, send_sem=sems.at[d, i], recv_sem=r_sem.at[d, i],
                device_id=(v, target), device_id_type=MESH)

        def send_own(u):
            @pl.when(has_r)
            def _():
                remote(o, u, s_right, right).start()

            @pl.when(has_l)
            def _():
                remote(o, u, s_left, left).start()

            remote(o, u, s_part, part).start()

        def relay(h, u):
            @pl.when(z - h >= 0)
            def _():
                d = (z - h) * CORES + k
                remote(d, u, s_right, right).wait_recv()

                @pl.when(has_r)
                def _():
                    remote(d, u, s_right, right).start()

                remote(d, u, s_part, part).start()

            @pl.when(z + h < NZ)
            def _():
                d = (z + h) * CORES + k
                remote(d, u, s_left, left).wait_recv()

                @pl.when(has_l)
                def _():
                    remote(d, u, s_left, left).start()

                remote(d, u, s_part, part).start()

        def from_partner(u):
            for s in range(NZ):
                remote(s * CORES + 1 - k, u, s_part, part).wait_recv()

        units = ["a", "t"] + list(range(Q))
        LEAD = 2 + SKEW * max(NZ - 2, 0)

        def finish(u):
            for s in range(NZ):
                d = s * CORES + k

                @pl.when(jnp.logical_and(s <= z, has_r))
                def _():
                    remote(d, u, s_right, right).wait_send()

                @pl.when(jnp.logical_and(s >= z, has_l))
                def _():
                    remote(d, u, s_left, left).wait_send()

                remote(d, u, s_part, part).wait_send()

        for u in units[:AHEAD]:
            send_own(u)

        @pl.loop(0, Q)
        def _(q):
            vin(q).start()

        for q in range(Q):
            for r in range(R):
                drows[r * Q + q:r * Q + q + 1, :] = oloc[q, r:r + 1, :]

        for t in range(LEAD):
            if AHEAD <= t + AHEAD < UNITS:
                send_own(units[t + AHEAD])
            for h in range(1, NZ):
                n = t - SKEW * (h - 1)
                if 0 <= n < UNITS:
                    relay(h, units[n])
        from_partner("a")

        def a_copy(h):
            w = lax.rem(v + h, W)
            return pltpu.make_async_remote_copy(
                src_ref=amps.at[v], dst_ref=amps.at[v], send_sem=a_s.at[h],
                recv_sem=a_r.at[h], device_id=(w, o), device_id_type=MESH)

        def a_came(h):
            w = lax.rem(v - h + W, W)
            return pltpu.make_async_remote_copy(
                src_ref=amps.at[w], dst_ref=amps.at[w], send_sem=a_s.at[h],
                recv_sem=a_r.at[h], device_id=(w, o), device_id_type=MESH)

        for h in range(1, W):
            a_copy(h).start()
        from_partner("t")

        xbuf[...] = jnp.zeros_like(xbuf)
        for h in range(1, W):
            a_came(h).wait_recv()
        for d in range(D):
            for j in range(NJ):
                at = d * R + j * GR
                for w in range(W):
                    xbuf[at:at + GR, w * PIECE:(w + 1) * PIECE] = amps[w, d, j]
        amp = xbuf[0:OCC, 0:A]
        tmat[...] = jnp.zeros_like(tmat)
        shifted = jnp.concatenate([jnp.zeros((OCC, OCC), F32), amp], axis=1)
        thi, tlo = split(shifted)
        tmat[0:OCC, :] = thi
        tmat[KP:KP + OCC, :] = tlo
        thi, tlo = split(jnp.transpose(xbuf[:, 0:AP])[0:A])
        tright[:, 0:KP] = thi
        tright[:, KP:2 * KP] = tlo
        ahi, alo = split(xbuf[:, 0:A])
        pick = (lax.broadcasted_iota(jnp.int32, (A, VP), 0)
                == lax.broadcasted_iota(jnp.int32, (A, VP), 1) + o * RV)
        pick = jnp.where(pick, 1.0, 0.0).astype(BF16)
        shi = dot(ahi, pick).astype(BF16)
        sleft[0:KP, 0:VP] = shi
        sleft[KP:2 * KP, 0:VP] = shi
        sleft[0:KP, VP:2 * VP] = dot(alo, pick).astype(BF16)
        sleft[KP:2 * KP, VP:2 * VP] = jnp.zeros((KP, VP), BF16)
        lwts[...] = jnp.zeros_like(lwts)

        keep = lax.broadcasted_iota(jnp.int32, (ROWS, KP), 1) < OCC
        hi, lo = split(jnp.where(keep, drows[:, 0:KP], 0.0))
        extra = dot(jnp.concatenate([hi, hi], axis=1), tmat[...]) + dot(lo, tmat[0:KP, :])
        drows[...] = drows[...] + extra
        for w in range(W):
            sl = drows[:, OCC + w * PIECE:OCC + (w + 1) * PIECE]
            for r in range(R):
                ovsend[w, r] = sl[r * Q:(r + 1) * Q]
        total = tails[0, GROUPS * NJ]
        for d in range(1, D):
            total = total + tails[d, GROUPS * NJ]
        rid = lax.broadcasted_iota(jnp.int32, (R, ROWS), 0) * Q
        cid = lax.broadcasted_iota(jnp.int32, (R, ROWS), 1)
        wts = jnp.zeros((R, ROWS), F32)
        for q in range(Q):
            wts = wts + jnp.where(cid == rid + q, jnp.broadcast_to(total[0:1, q:q + 1], (R, ROWS)), 0.0)
        whi, wlo = split(wts)
        dhi, dlo = split(drows[...])
        fock = (dot(whi, dhi) + (dot(whi, dlo) + dot(wlo, dhi)))[:, OCC:]
        for j in range(NJ):
            fbuf[v, j] = fock[j * GR:(j + 1) * GR]

        def ov_copy(h):
            w = lax.rem(v + h, W)
            return pltpu.make_async_remote_copy(
                src_ref=ovsend.at[w], dst_ref=ovrecv.at[v], send_sem=ov_s.at[h],
                recv_sem=ov_r.at[h], device_id=(w, o), device_id_type=MESH)

        def f_copy(h):
            w = lax.rem(v + h, W)
            return pltpu.make_async_remote_copy(
                src_ref=fbuf.at[v], dst_ref=fbuf.at[v], send_sem=f_s.at[h],
                recv_sem=f_r.at[h], device_id=(w, o), device_id_type=MESH)

        for h in range(1, W):
            ov_copy(h).start()
            f_copy(h).start()
        ovrecv[v] = ovsend[v]

        @pl.loop(0, Q)
        def _(q):
            @pl.when(q + LEAD + AHEAD < UNITS)
            def _():
                send_own(q + LEAD + AHEAD - 2)

            for h in range(1, NZ):
                n = q + LEAD - SKEW * (h - 1)

                @pl.when(n < UNITS)
                def _():
                    relay(h, n - 2)

            from_partner(q)
            if TAIL:
                shift = lax.rem(LANES - lax.rem(q, SLOTS) * TAIL, LANES)
            for d in range(D):
                for j in range(NJ):
                    at = d * R + j * GR
                    xbuf[at:at + GR, 0:MAIN] = gath[d, q * NJ + j]
                    if TAIL:
                        t = pltpu.roll(tails[d, (q // SLOTS) * NJ + j], shift, axis=1)
                        xbuf[at:at + GR, MAIN:N] = t[:, 0:TAIL]
            hi, lo = split(jnp.transpose(xbuf[...])[0:N])
            prod = dot(jnp.concatenate([hi, lo], axis=1), sleft[...])
            prod = prod[:, 0:VP] + prod[:, VP:2 * VP]
            vin(q).wait()
            vloc[q] = vloc[q] - prod[:, 0:RV]
            hi, lo = split(vloc[q, 0:OCC, :])
            lwts[0:OCC, 0:RV] = hi
            lwts[KP:KP + OCC, 0:RV] = hi
            lwts[0:OCC, VP:VP + RV] = lo
            prod = dot(tright[...], lwts[...])
            prod = prod[:, 0:VP] + prod[:, VP:2 * VP]
            vloc[q, OCC:N, :] = vloc[q, OCC:N, :] + prod[:, 0:RV]
            vout(q).start()

        for h in range(1, W):
            ov_copy(h).wait_recv()
            f_copy(h).wait_recv()
        for w in range(W):
            for r in range(R):
                ovout[r, w * Q:(w + 1) * Q, :] = ovrecv[w, r]
        c_ov = pltpu.make_async_copy(ovout, out_ov, o_out.at[0])
        c_ov.start()
        for j in range(NJ):
            acc = fbuf[0, j]
            for w in range(1, W):
                acc = acc + fbuf[w, j]
            fout[j * GR:(j + 1) * GR, :] = acc / (Q * W)
        c_f = pltpu.make_async_copy(fout, out_fock, o_out.at[1])
        c_f.start()

        finish("a")
        finish("t")

        @pl.loop(0, Q)
        def _(u):
            finish(u)
            vout(u).wait()

        for h in range(1, W):
            ov_copy(h).wait_send()
            f_copy(h).wait_send()
            a_copy(h).wait_send()
        c_ov.wait()
        c_f.wait()

    DMA = pltpu.SemaphoreType.DMA
    V = pltpu.VMEM
    any_spec = pl.BlockSpec(memory_space=pl.ANY)
    return pl.pallas_call(
        kernel,
        name="dress",
        out_shape=(jax.ShapeDtypeStruct((Q, N, RV), F32),
                   jax.ShapeDtypeStruct((R, Q * W, PIECE), F32),
                   jax.ShapeDtypeStruct((R, A), F32)),
        in_specs=[pl.BlockSpec(memory_space=pltpu.HBM)] * 3,
        out_specs=(any_spec,) * 3,
        scratch_shapes=[
            V((D, GRAN, GR, MAIN), F32),
            V((W, D, NJ, GR, PIECE), F32),
            V((D, GROUPS * NJ + 1, GR, LANES), F32),
            V((Q, N, RV), F32),
            V((Q, R, N), F32),
            V((R, A), F32),
            V((KP, NP), F32),
            V((ROWS, N), F32),
            V((2 * KP, N), BF16),
            V((A, 2 * KP), BF16),
            V((2 * KP, 2 * VP), BF16),
            V((2 * KP, 2 * VP), BF16),
            V((W, R, Q, PIECE), F32),
            V((W, R, Q, PIECE), F32),
            V((R, Q * W, PIECE), F32),
            V((W, NJ, GR, A), F32),
            V((R, A), F32),
            DMA((D, UNITS)), DMA((D, UNITS)), DMA((D, UNITS)), DMA((D, UNITS)),
            DMA((W,)), DMA((W,)), DMA((W,)), DMA((W,)), DMA((W,)), DMA((W,)),
            DMA((2,)), DMA((Q,)), DMA((Q,)), DMA((2,)),
        ],
        compiler_params=pltpu.CompilerParams(
            collective_id=0, has_side_effects=True, vmem_limit_bytes=40 * 2**20),
    )


def write_out(*refs):
    n = (len(refs) - 1) // 2
    copies = [pltpu.make_async_copy(refs[i], refs[n + i], refs[-1].at[i]) for i in range(n)]
    for c in copies:
        c.start()
    for c in copies:
        c.wait()


def store(arrays):
    return pl.pallas_call(
        write_out,
        name="store",
        out_shape=tuple(jax.ShapeDtypeStruct(a.shape, a.dtype) for a in arrays),
        in_specs=[pl.BlockSpec(memory_space=pl.ANY)] * len(arrays),
        out_specs=(pl.BlockSpec(memory_space=pltpu.HBM),) * len(arrays),
        scratch_shapes=[pltpu.SemaphoreType.DMA((len(arrays),))],
        compiler_params=pltpu.CompilerParams(vmem_limit_bytes=2**20),
    )(*arrays)


def solution(mesh):
    W, D = mesh.shape["vec"], mesh.shape["orb"]

    def shards(chol_occ, chol_vir, singles):
        Q, R, N = chol_occ.shape
        call = make_kernel(W, D, Q, R, chol_vir.shape[1], N, singles.shape[1])
        args = (chol_occ, jnp.swapaxes(chol_vir, 1, 2), singles)
        vir, ov, fock = store(call(*(pltpu.with_memory_space_constraint(a, pltpu.HBM) for a in args)))
        return jnp.swapaxes(vir, 1, 2), jnp.swapaxes(ov, 0, 1), fock

    return jax.shard_map(
        shards,
        mesh=mesh,
        in_specs=(P("vec", "orb", None), P("vec", "orb", None), P("orb", None)),
        out_specs=(P("vec", "orb", None), P(None, "orb", "vec"), P("orb", None)),
        check_vma=False,
    )
```

```python
import jax
import jax.numpy as jnp
from jax import lax
from jax.experimental import pallas as pl
from jax.experimental.pallas import tpu as pltpu
from jax.sharding import PartitionSpec as P

MESH = pl.DeviceIdType.MESH
F32, BF16 = jnp.float32, jnp.bfloat16
LANES = 128
CORES = 2
SKEW = 1
AHEAD = 4


def split(x):
    hi = x.astype(BF16)
    return hi, (x - hi.astype(F32)).astype(BF16)


def dot(a, b):
    return jnp.dot(a, b, preferred_element_type=F32)


def make_kernel(W, D, Q, R, RV, N, A):
    OCC = N - A
    NZ = D // CORES
    GR = 8 if R % 8 == 0 else (4 if R % 4 == 0 else R)
    NJ = R // GR
    ROWS = Q * R
    GRAN = Q * NJ
    MAIN = N // LANES * LANES
    TAIL = N - MAIN
    SLOTS = LANES // TAIL if TAIL else 1
    GROUPS = -(-Q // SLOTS)
    PIECE = A // W
    KP = -(-OCC // LANES) * LANES
    UNITS = Q + 2
    NP = -(-N // LANES) * LANES
    AP = -(-A // LANES) * LANES
    VP = -(-RV // LANES) * LANES

    def kernel(occ, vir, sing, out_vir, out_ov, out_fock,
               gath, amps, tails, vloc, oloc, sloc, xbuf, drows, tmat, tright, sleft, lwts,
               ovsend, ovrecv, ovout, fbuf, fout,
               s_right, s_left, s_part, r_sem, ov_s, ov_r, f_s, f_r, in_sem, v_in, v_out, o_out):
        v = lax.axis_index("vec")
        o = lax.axis_index("orb")
        z = o // CORES
        k = o % CORES
        has_r = z < NZ - 1
        has_l = z > 0
        right = lax.rem(o + CORES, D)
        left = lax.rem(o - CORES + D, D)
        part = z * CORES + (1 - k)

        c_occ = pltpu.make_async_copy(occ, oloc, in_sem.at[0])
        c_sing = pltpu.make_async_copy(sing, sloc, in_sem.at[1])
        c_occ.start()
        c_sing.start()

        def vin(q):
            return pltpu.make_async_copy(vir.at[q], vloc.at[q], v_in.at[q])

        def vout(q):
            return pltpu.make_async_copy(vloc.at[q], out_vir.at[q], v_out.at[q])

        bar = pltpu.get_barrier_semaphore()

        @pl.when(has_r)
        def _():
            pl.semaphore_signal(bar, inc=1, device_id=(v, right), device_id_type=MESH)

        @pl.when(has_l)
        def _():
            pl.semaphore_signal(bar, inc=1, device_id=(v, left), device_id_type=MESH)

        pl.semaphore_signal(bar, inc=1, device_id=(v, part), device_id_type=MESH)
        for h in range(1, W):
            pl.semaphore_signal(bar, inc=1, device_id=(lax.rem(v + h, W), o), device_id_type=MESH)

        c_occ.wait()
        c_sing.wait()
        for j in range(NJ):
            amps[o, j] = sloc[j * GR:(j + 1) * GR, :]
        for q in range(Q):
            for j in range(NJ):
                gath[o, q * NJ + j] = oloc[q, j * GR:(j + 1) * GR, 0:MAIN]
        if TAIL:
            for g in range(GROUPS):
                parts = [oloc[min(g * SLOTS + t, Q - 1), :, MAIN:N] for t in range(SLOTS)]
                packed = jnp.concatenate(parts, axis=1) if SLOTS > 1 else parts[0]
                for j in range(NJ):
                    tails[o, g * NJ + j, :, 0:SLOTS * TAIL] = packed[j * GR:(j + 1) * GR]
        ri = lax.broadcasted_iota(jnp.int32, (R, KP), 0) + o * R
        ci = lax.broadcasted_iota(jnp.int32, (R, KP), 1)
        mask = ri == ci
        lane = lax.broadcasted_iota(jnp.int32, (GR, LANES), 1)
        tr = jnp.zeros((GR, LANES), F32)
        for q in range(Q):
            dq = jnp.sum(jnp.where(mask, oloc[q, :, 0:KP], 0.0), axis=0, keepdims=True)
            tq = jnp.sum(dq, axis=1, keepdims=True)
            tr = tr + jnp.where(lane == q, jnp.broadcast_to(tq, (GR, LANES)), 0.0)
        tails[o, GROUPS * NJ] = tr

        pl.semaphore_wait(bar, has_r.astype(jnp.int32) + has_l.astype(jnp.int32) + W)

        def piece(d, u):
            if isinstance(u, str):
                return {"a": amps, "t": tails}[u].at[d], {"a": Q, "t": Q + 1}[u]
            return gath.at[d, pl.ds(u * NJ, NJ)], u

        def remote(d, u, sems, target):
            ref, i = piece(d, u)
            return pltpu.make_async_remote_copy(
                src_ref=ref, dst_ref=ref, send_sem=sems.at[d, i], recv_sem=r_sem.at[d, i],
                device_id=(v, target), device_id_type=MESH)

        def send_own(u):
            @pl.when(has_r)
            def _():
                remote(o, u, s_right, right).start()

            @pl.when(has_l)
            def _():
                remote(o, u, s_left, left).start()

            remote(o, u, s_part, part).start()

        def relay(h, u):
            @pl.when(z - h >= 0)
            def _():
                d = (z - h) * CORES + k
                remote(d, u, s_right, right).wait_recv()

                @pl.when(has_r)
                def _():
                    remote(d, u, s_right, right).start()

                remote(d, u, s_part, part).start()

            @pl.when(z + h < NZ)
            def _():
                d = (z + h) * CORES + k
                remote(d, u, s_left, left).wait_recv()

                @pl.when(has_l)
                def _():
                    remote(d, u, s_left, left).start()

                remote(d, u, s_part, part).start()

        def from_partner(u):
            for s in range(NZ):
                remote(s * CORES + 1 - k, u, s_part, part).wait_recv()

        units = ["a", "t"] + list(range(Q))
        LEAD = 2 + SKEW * max(NZ - 2, 0)

        def finish(u):
            for s in range(NZ):
                d = s * CORES + k

                @pl.when(jnp.logical_and(s <= z, has_r))
                def _():
                    remote(d, u, s_right, right).wait_send()

                @pl.when(jnp.logical_and(s >= z, has_l))
                def _():
                    remote(d, u, s_left, left).wait_send()

                remote(d, u, s_part, part).wait_send()

        for u in units[:AHEAD]:
            send_own(u)

        @pl.loop(0, Q)
        def _(q):
            vin(q).start()

        for q in range(Q):
            for r in range(R):
                drows[r * Q + q:r * Q + q + 1, :] = oloc[q, r:r + 1, :]

        for t in range(LEAD):
            if AHEAD <= t + AHEAD < UNITS:
                send_own(units[t + AHEAD])
            for h in range(1, NZ):
                n = t - SKEW * (h - 1)
                if 0 <= n < UNITS:
                    relay(h, units[n])
        from_partner("a")
        from_partner("t")

        xbuf[...] = jnp.zeros_like(xbuf)
        for d in range(D):
            for j in range(NJ):
                at = d * R + j * GR
                xbuf[at:at + GR, 0:A] = amps[d, j]
        amp = xbuf[0:OCC, 0:A]
        tmat[...] = jnp.zeros_like(tmat)
        shifted = jnp.concatenate([jnp.zeros((OCC, OCC), F32), amp], axis=1)
        thi, tlo = split(shifted)
        tmat[0:OCC, :] = thi
        tmat[KP:KP + OCC, :] = tlo
        thi, tlo = split(jnp.transpose(xbuf[:, 0:AP])[0:A])
        tright[:, 0:KP] = thi
        tright[:, KP:2 * KP] = tlo
        ahi, alo = split(xbuf[:, 0:A])
        pick = (lax.broadcasted_iota(jnp.int32, (A, VP), 0)
                == lax.broadcasted_iota(jnp.int32, (A, VP), 1) + o * RV)
        pick = jnp.where(pick, 1.0, 0.0).astype(BF16)
        shi = dot(ahi, pick).astype(BF16)
        sleft[0:KP, 0:VP] = shi
        sleft[KP:2 * KP, 0:VP] = shi
        sleft[0:KP, VP:2 * VP] = dot(alo, pick).astype(BF16)
        sleft[KP:2 * KP, VP:2 * VP] = jnp.zeros((KP, VP), BF16)
        lwts[...] = jnp.zeros_like(lwts)

        keep = lax.broadcasted_iota(jnp.int32, (ROWS, KP), 1) < OCC
        hi, lo = split(jnp.where(keep, drows[:, 0:KP], 0.0))
        extra = dot(jnp.concatenate([hi, hi], axis=1), tmat[...]) + dot(lo, tmat[0:KP, :])
        drows[...] = drows[...] + extra
        for w in range(W):
            sl = drows[:, OCC + w * PIECE:OCC + (w + 1) * PIECE]
            for r in range(R):
                ovsend[w, r] = sl[r * Q:(r + 1) * Q]
        total = tails[0, GROUPS * NJ]
        for d in range(1, D):
            total = total + tails[d, GROUPS * NJ]
        rid = lax.broadcasted_iota(jnp.int32, (R, ROWS), 0) * Q
        cid = lax.broadcasted_iota(jnp.int32, (R, ROWS), 1)
        wts = jnp.zeros((R, ROWS), F32)
        for q in range(Q):
            wts = wts + jnp.where(cid == rid + q, jnp.broadcast_to(total[0:1, q:q + 1], (R, ROWS)), 0.0)
        whi, wlo = split(wts)
        dhi, dlo = split(drows[...])
        fock = (dot(whi, dhi) + (dot(whi, dlo) + dot(wlo, dhi)))[:, OCC:]
        for j in range(NJ):
            fbuf[v, j] = fock[j * GR:(j + 1) * GR]

        def ov_copy(h):
            w = lax.rem(v + h, W)
            return pltpu.make_async_remote_copy(
                src_ref=ovsend.at[w], dst_ref=ovrecv.at[v], send_sem=ov_s.at[h],
                recv_sem=ov_r.at[h], device_id=(w, o), device_id_type=MESH)

        def f_copy(h):
            w = lax.rem(v + h, W)
            return pltpu.make_async_remote_copy(
                src_ref=fbuf.at[v], dst_ref=fbuf.at[v], send_sem=f_s.at[h],
                recv_sem=f_r.at[h], device_id=(w, o), device_id_type=MESH)

        for h in range(1, W):
            ov_copy(h).start()
            f_copy(h).start()
        ovrecv[v] = ovsend[v]

        @pl.loop(0, Q)
        def _(q):
            @pl.when(q + LEAD + AHEAD < UNITS)
            def _():
                send_own(q + LEAD + AHEAD - 2)

            for h in range(1, NZ):
                n = q + LEAD - SKEW * (h - 1)

                @pl.when(n < UNITS)
                def _():
                    relay(h, n - 2)

            from_partner(q)
            if TAIL:
                shift = lax.rem(LANES - lax.rem(q, SLOTS) * TAIL, LANES)
            for d in range(D):
                for j in range(NJ):
                    at = d * R + j * GR
                    xbuf[at:at + GR, 0:MAIN] = gath[d, q * NJ + j]
                    if TAIL:
                        t = pltpu.roll(tails[d, (q // SLOTS) * NJ + j], shift, axis=1)
                        xbuf[at:at + GR, MAIN:N] = t[:, 0:TAIL]
            hi, lo = split(jnp.transpose(xbuf[...])[0:N])
            prod = dot(jnp.concatenate([hi, lo], axis=1), sleft[...])
            prod = prod[:, 0:VP] + prod[:, VP:2 * VP]
            vin(q).wait()
            vloc[q] = vloc[q] - prod[:, 0:RV]
            hi, lo = split(vloc[q, 0:OCC, :])
            lwts[0:OCC, 0:RV] = hi
            lwts[KP:KP + OCC, 0:RV] = hi
            lwts[0:OCC, VP:VP + RV] = lo
            prod = dot(tright[...], lwts[...])
            prod = prod[:, 0:VP] + prod[:, VP:2 * VP]
            vloc[q, OCC:N, :] = vloc[q, OCC:N, :] + prod[:, 0:RV]
            vout(q).start()

        for h in range(1, W):
            ov_copy(h).wait_recv()
            f_copy(h).wait_recv()
        for w in range(W):
            for r in range(R):
                ovout[r, w * Q:(w + 1) * Q, :] = ovrecv[w, r]
        c_ov = pltpu.make_async_copy(ovout, out_ov, o_out.at[0])
        c_ov.start()
        for j in range(NJ):
            acc = fbuf[0, j]
            for w in range(1, W):
                acc = acc + fbuf[w, j]
            fout[j * GR:(j + 1) * GR, :] = acc / (Q * W)
        c_f = pltpu.make_async_copy(fout, out_fock, o_out.at[1])
        c_f.start()

        finish("a")
        finish("t")

        @pl.loop(0, Q)
        def _(u):
            finish(u)
            vout(u).wait()

        for h in range(1, W):
            ov_copy(h).wait_send()
            f_copy(h).wait_send()
        c_ov.wait()
        c_f.wait()

    DMA = pltpu.SemaphoreType.DMA
    V = pltpu.VMEM
    any_spec = pl.BlockSpec(memory_space=pl.ANY)
    return pl.pallas_call(
        kernel,
        name="dress",
        out_shape=(jax.ShapeDtypeStruct((Q, N, RV), F32),
                   jax.ShapeDtypeStruct((R, Q * W, PIECE), F32),
                   jax.ShapeDtypeStruct((R, A), F32)),
        in_specs=[pl.BlockSpec(memory_space=pltpu.HBM)] * 3,
        out_specs=(any_spec,) * 3,
        scratch_shapes=[
            V((D, GRAN, GR, MAIN), F32),
            V((D, NJ, GR, A), F32),
            V((D, GROUPS * NJ + 1, GR, LANES), F32),
            V((Q, N, RV), F32),
            V((Q, R, N), F32),
            V((R, A), F32),
            V((KP, NP), F32),
            V((ROWS, N), F32),
            V((2 * KP, N), BF16),
            V((A, 2 * KP), BF16),
            V((2 * KP, 2 * VP), BF16),
            V((2 * KP, 2 * VP), BF16),
            V((W, R, Q, PIECE), F32),
            V((W, R, Q, PIECE), F32),
            V((R, Q * W, PIECE), F32),
            V((W, NJ, GR, A), F32),
            V((R, A), F32),
            DMA((D, UNITS)), DMA((D, UNITS)), DMA((D, UNITS)), DMA((D, UNITS)),
            DMA((W,)), DMA((W,)), DMA((W,)), DMA((W,)),
            DMA((2,)), DMA((Q,)), DMA((Q,)), DMA((2,)),
        ],
        compiler_params=pltpu.CompilerParams(
            collective_id=0, has_side_effects=True, vmem_limit_bytes=40 * 2**20),
    )


def write_out(*refs):
    n = (len(refs) - 1) // 2
    copies = [pltpu.make_async_copy(refs[i], refs[n + i], refs[-1].at[i]) for i in range(n)]
    for c in copies:
        c.start()
    for c in copies:
        c.wait()


def store(arrays):
    return pl.pallas_call(
        write_out,
        name="store",
        out_shape=tuple(jax.ShapeDtypeStruct(a.shape, a.dtype) for a in arrays),
        in_specs=[pl.BlockSpec(memory_space=pl.ANY)] * len(arrays),
        out_specs=(pl.BlockSpec(memory_space=pltpu.HBM),) * len(arrays),
        scratch_shapes=[pltpu.SemaphoreType.DMA((len(arrays),))],
        compiler_params=pltpu.CompilerParams(vmem_limit_bytes=2**20),
    )(*arrays)


def solution(mesh):
    W, D = mesh.shape["vec"], mesh.shape["orb"]

    def shards(chol_occ, chol_vir, singles):
        Q, R, N = chol_occ.shape
        call = make_kernel(W, D, Q, R, chol_vir.shape[1], N, singles.shape[1])
        args = (chol_occ, jnp.swapaxes(chol_vir, 1, 2), singles)
        vir, ov, fock = store(call(*(pltpu.with_memory_space_constraint(a, pltpu.HBM) for a in args)))
        return jnp.swapaxes(vir, 1, 2), jnp.swapaxes(ov, 0, 1), fock

    return jax.shard_map(
        shards,
        mesh=mesh,
        in_specs=(P("vec", "orb", None), P("vec", "orb", None), P("orb", None)),
        out_specs=(P("vec", "orb", None), P(None, "orb", "vec"), P("orb", None)),
        check_vma=False,
    )
```
